256 devices in a mesh: row: 16 (over y, z_lo, core), col: 16 (over x, z_hi).
Axes of the slice: x: 4, y: 4, z: 8 (z_hi: 4, z_lo: 2; z = z_hi * 2 + z_lo), core: 2. Of those that a mesh axis runs over, the one named last changes fastest.
Arguments:
- fisher: float32 [16384, 16384], P('row', 'col'), may hold values from -6 to 6
- slab: float32 [2048, 16384], P(('row', 'col')), may hold values from -6 to 6
Outputs:
- fisher_out: float32 [16384, 16384], P('row', 'col')
The draws below stay inside these ranges and needn't reach their ends.
All inputs are finite; a program needn't handle non-finite values.
Results may differ from the reference program's by a relative error of at most 0.00005.
Values sent between devices are 32-bit elements; how exact they have to be, the bound alone decides.
No kernel may reach another device: no remote copies, remote signals or barrier semaphores. Data moves between devices by JAX's collectives and lax.ppermute only.
A program may use at most 128 MiB of HBM per device.

```python
import jax
import jax.numpy as jnp
from jax import lax

ORDER = 16384
EXAMPLES = 2048


def block_scale(stream_key, extent, shards, smallest, largest):
    factor_of, own = 1.0, jax.random.fold_in(stream_key, 6)
    for position, shards_of in shards:
        steps = jnp.exp(jax.random.uniform(jax.random.fold_in(own, position), (shards_of,), jnp.float32, smallest / len(shards), largest / len(shards)))
        factor_of = factor_of * jnp.repeat(steps, extent[position] // shards_of).reshape([-1 if axis == position else 1 for axis in range(len(extent))])
    return factor_of


def scatter_about(stream_key, extent, scale, most, cuts=(), kind=jnp.bfloat16):
    drawn = scale * jax.random.normal(stream_key, extent, jnp.float32)
    if cuts:
        drawn = drawn * block_scale(stream_key, extent, cuts, -0.22, 0.18)
    return jnp.clip(drawn, -most, most).astype(kind)


def setup_inputs(seed: int = 0) -> dict:
    keys = jax.random.split(jax.random.key(seed), 3)
    fisher = scatter_about(keys[0], (ORDER, ORDER), 1.0, 6.0, ((0, 16), (1, 16)), jnp.float32)
    slab = scatter_about(keys[1], (EXAMPLES, ORDER), 1.0, 6.0, ((0, 256),), jnp.float32)
    return dict(fisher=fisher, slab=slab)


def reference(fisher, slab):
    product = lax.dot_general(slab, slab, (((0,), (0,)), ((), ())), precision=lax.Precision.HIGHEST, preferred_element_type=jnp.float32)
    return fisher + product / EXAMPLES
```

```python
import functools

import jax
import jax.numpy as jnp
from jax import lax
from jax.experimental import pallas as pl
from jax.experimental.pallas import tpu as pltpu
from jax.sharding import PartitionSpec as P


AXES = ("row", "col")
TILE_N = 512


def send(value, dy=0, dzl=0, dk=0, dx=0, dzh=0):
    pairs = []
    for y in range(4):
        for zl in range(2):
            for k in range(2):
                for x in range(4):
                    for zh in range(4):
                        here = (y * 4 + zl * 2 + k) * 16 + x * 4 + zh
                        there = (((y + dy) % 4) * 4 + (zl ^ dzl) * 2 + (k ^ dk)) * 16
                        there += ((x + dx) % 4) * 4 + (zh + dzh) % 4
                        pairs.append((there, here))
    return lax.ppermute(value, AXES, pairs)


def split(value):
    high = value.astype(jnp.bfloat16)
    return high, (value - high.astype(jnp.float32)).astype(jnp.bfloat16)


def kernel(row_classes, where_c, where_r, n_left, scale, place, acc, *refs):
    col_sets = len(where_r)
    left, right = refs[:n_left], refs[n_left : n_left + col_sets]
    r, c = place[0], place[1]
    from_row = [(((r >> 2) + dy) & 3) * 4 + (((r >> 1) & 1) ^ dzl) * 2 + ((r & 1) ^ dk) for dy, dzl, dk in where_r]
    from_col = [(((c >> 2) + dx) & 3) * 4 + (((c & 3) + dzh) & 3) for dx, dzh in where_c]
    out, lh, ll, rh, rl = refs[n_left + col_sets :]
    depth = 8 * col_sets

    @pl.when(pl.program_id(0) == 0)
    def _():
        for b, (which, base) in enumerate(row_classes):
            for pair in range(col_sets // 2):
                two = jnp.concatenate([left[which][base + from_row[2 * pair]], left[which][base + from_row[2 * pair + 1]]], axis=0)
                rows = pl.ds(b * depth + pair * 16, 16)
                lh[rows, :], ll[rows, :] = split(two)

    for b, at in enumerate(from_col):
        for pair in range(col_sets // 2):
            two = jnp.concatenate([right[2 * pair][at], right[2 * pair + 1][at]], axis=0)
            rows = pl.ds(b * depth + pair * 16, 16)
            rh[rows, :], rl[rows, :] = split(two)

    dims = (((0,), (0,)), ((), ()))
    dot = functools.partial(lax.dot_general, dimension_numbers=dims, preferred_element_type=jnp.float32)
    total = dot(lh[...], rh[...]) + dot(ll[...], rh[...]) + dot(lh[...], rl[...])
    out[...] = acc[...] + total * scale


def accumulate(acc, left, row_classes, where_c, right, where_r, place, scale):
    m, n = acc.shape
    tile = min(TILE_N, n)
    k = 8 * len(right) * len(row_classes)
    grid_spec = pltpu.PrefetchScalarGridSpec(
        num_scalar_prefetch=1,
        grid=(n // tile,),
        in_specs=[pl.BlockSpec((m, tile), lambda j, t: (0, j))]
        + [pl.BlockSpec(v.shape, lambda j, t: (0, 0, 0), pipeline_mode=pl.Buffered(1)) for v in left]
        + [pl.BlockSpec((v.shape[0], 8, tile), lambda j, t: (0, 0, j)) for v in right],
        out_specs=pl.BlockSpec((m, tile), lambda j, t: (0, j)),
        scratch_shapes=[pltpu.VMEM((k, m), jnp.bfloat16)] * 2 + [pltpu.VMEM((k, tile), jnp.bfloat16)] * 2,
    )
    return pl.pallas_call(
        functools.partial(kernel, row_classes, where_c, where_r, len(left), scale),
        out_shape=jax.ShapeDtypeStruct(acc.shape, acc.dtype),
        grid_spec=grid_spec,
        cost_estimate=pl.CostEstimate(flops=6 * m * n * k, bytes_accessed=4 * k * (m + n) + 8 * m * n, transcendentals=0),
        compiler_params=pltpu.CompilerParams(vmem_limit_bytes=56 << 20),
    )(place, acc, *left, *right)


def step(fisher, slab):
    n_row, n_col = lax.axis_size("row"), lax.axis_size("col")
    rows, order = slab.shape
    t_row, t_col = order // n_row, order // n_col
    scale = 1.0 / (rows * n_row * n_col)
    place = jnp.stack([lax.axis_index("row"), lax.axis_index("col")])

    def exchange(axis, n, t, slab):
        got = lax.all_to_all(slab.reshape(rows, n, t), axis, split_axis=1, concat_axis=1, tiled=True)
        return got.transpose(1, 0, 2)

    s = exchange("row", n_row, t_row, slab)
    xp, xm, x2 = send(s, dx=1), send(s, dx=-1), send(s, dx=2)
    zp, zm = send(s, dzh=1), send(s, dzh=-1)
    d = exchange("col", n_col, t_col, slab)
    z2 = send(s, dzh=2)
    b = jnp.concatenate([zp, zm], axis=0)
    bp, bm = send(b, dx=1), send(b, dx=-1)
    b2p, b2m = send(bp[:16], dx=1), send(bm[16:], dx=-1)
    cp, cm = send(z2, dx=1), send(z2, dx=-1)
    c2p, c2m = send(cp[:8], dx=1), send(cm[8:], dx=-1)

    dl = send(d, dzl=1)
    dp, dm = send(d, dy=1), send(d, dy=-1)
    lp, lm = send(dl, dy=1), send(dl, dy=-1)
    d2, l2 = send(dp, dy=1), send(lm, dy=-1)
    own = [(d, 0, 0), (dl, 0, 1), (dp, 1, 0), (dm, -1, 0), (lp, 1, 1), (lm, -1, 1), (d2, 2, 0), (l2, 2, 1)]
    right, where_r = [], []
    for value, dy, dzl in own:
        right += [value, send(value, dk=1)]
        where_r += [(dy, dzl, 0), (dy, dzl, 1)]

    def add(acc, left, row_classes, where_c):
        return accumulate(acc, left, row_classes, where_c, right, where_r, place, scale)

    acc = add(
        fisher,
        [s, xp, xm, x2, b, z2, bp, bm],
        [(0, 0), (1, 0), (2, 0), (3, 0), (4, 0), (4, 16), (5, 0), (6, 0), (6, 16), (7, 0), (7, 16)],
        [(0, 0), (1, 0), (-1, 0), (2, 0), (0, 1), (0, -1), (0, 2), (1, 1), (1, -1), (-1, 1), (-1, -1)],
    )
    acc = add(acc, [b2p, b2m, cp, cm], [(0, 0), (1, 0), (2, 0), (3, 0)], [(2, 1), (2, -1), (1, 2), (-1, 2)])
    acc, c2p, c2m = lax.optimization_barrier((acc, c2p, c2m))
    return add(acc, [jnp.concatenate([c2p, c2m], axis=0)], [(0, 0)], [(2, 2)])


def solution(mesh):
    return jax.shard_map(
        step,
        mesh=mesh,
        in_specs=(P("row", "col"), P(("row", "col"), None)),
        out_specs=P("row", "col"),
        check_vma=False,
    )
```

```python
import functools

import jax
import jax.numpy as jnp
from jax import lax
from jax.experimental import pallas as pl
from jax.experimental.pallas import tpu as pltpu
from jax.sharding import PartitionSpec as P


AXES = ("row", "col")
TILE_N = 512
VMEM_BYTES = 24 << 20
INSIDE = pl.BlockSpec(memory_space=pltpu.VMEM)

SOURCES = (
    [(0, 0), (1, 0), (-1, 0), (2, 0), (0, 1), (0, -1), (1, 1), (-1, 1), (1, -1), (-1, -1), (0, 2)],
    [(2, 1), (2, -1), (1, 2), (-1, 2)],
    [(2, 2)],
)

STEPS = (0, 1, -1, 2)


def send(value, dy=0, dzl=0, dk=0, dx=0, dzh=0):
    def of(offset, k):
        return offset[k] if isinstance(offset, tuple) else offset

    pairs = []
    for y in range(4):
        for zl in range(2):
            for k in range(2):
                for x in range(4):
                    for zh in range(4):
                        here = (y * 4 + zl * 2 + k) * 16 + x * 4 + zh
                        there = (((y + of(dy, k)) % 4) * 4 + (zl ^ dzl) * 2 + (k ^ dk)) * 16
                        there += ((x + of(dx, k)) % 4) * 4 + (zh + of(dzh, k)) % 4
                        pairs.append((there, here))
    return lax.ppermute(value, AXES, pairs)


def relay(plus, minus, axis):
    value = jnp.where(lax.axis_index("row") & 1 == 0, plus, minus)
    return send(value, **{axis: (1, -1)})


def exchange(slab, axis):
    rows, order = slab.shape
    n = lax.axis_size(axis)
    got = lax.all_to_all(slab.reshape(rows, n, order // n), axis, split_axis=1, concat_axis=1, tiled=True)
    return got.transpose(1, 0, 2)


def split(value):
    high = value.astype(jnp.bfloat16)
    return high, (value - high.astype(jnp.float32)).astype(jnp.bfloat16)


def prepare_kernel(place, *refs):
    pieces, outs = refs[:8], refs[8:]
    c = place[1]
    width = 256

    @pl.loop(0, pieces[0].shape[2] // width)
    def _(j):
        cols = pl.ds(pl.multiple_of(j * width, width), width)
        for group, sources in enumerate(SOURCES):
            high, low = outs[2 * group : 2 * group + 2]
            for b, (dx, dzh) in enumerate(sources):
                at = (((c >> 2) + dx) & 3) * 4 + (((c & 3) + dzh) & 3)
                for i in range(4):
                    rows = pl.ds(b * 64 + i * 16, 16)
                    both = jnp.concatenate([pieces[2 * i][at, :, cols], pieces[2 * i + 1][at, :, cols]], axis=0)
                    high[rows, cols], low[rows, cols] = split(both)


def prepare(pieces, place):
    m = pieces[0].shape[2]
    ks = [64 * len(sources) for sources in SOURCES for _ in range(2)]
    return pl.pallas_call(
        prepare_kernel,
        out_shape=[jax.ShapeDtypeStruct((k, m), jnp.bfloat16) for k in ks],
        in_specs=[pl.BlockSpec(memory_space=pltpu.SMEM)] + [INSIDE] * len(pieces),
        out_specs=[INSIDE] * len(ks),
        cost_estimate=pl.CostEstimate(flops=2 * sum(ks) * m, bytes_accessed=4 * sum(ks) * m, transcendentals=0),
        compiler_params=pltpu.CompilerParams(vmem_limit_bytes=VMEM_BYTES),
    )(place, *pieces)


def product_kernel(parts, n_left, scale, last, place, acc, *refs):
    left, right = refs[:n_left], refs[n_left : n_left + 2 * len(parts)]
    out, *scratch = refs[n_left + 2 * len(parts) :]
    m, n = acc.shape
    width = 256
    dims = (((0,), (0,)), ((), ()))
    dot = functools.partial(lax.dot_general, dimension_numbers=dims, preferred_element_type=jnp.float32)

    r = place[0]
    y, k = r >> 2, r & 1

    def pieces(cols):
        at = 0
        for half, classes in parts:
            zl = ((r >> 1) & 1) ^ half
            for which in classes:
                for dy in STEPS:
                    group = ((y + dy) & 3) * 4 + zl * 2
                    both = [left[which][group + (k ^ dk), :, cols] for dk in (0, 1)]
                    yield pl.ds(at, 16), jnp.concatenate(both, axis=0)
                    at += 16

    if not last:
        lh, ll = scratch

        @pl.loop(0, m // width)
        def _(j):
            cols = pl.ds(pl.multiple_of(j * width, width), width)
            for rows, value in pieces(cols):
                lh[rows, cols], ll[rows, cols] = split(value)

        @pl.loop(0, n // TILE_N)
        def _(j):
            cols = pl.ds(pl.multiple_of(j * TILE_N, TILE_N), TILE_N)
            at, total = 0, None
            for i in range(len(parts)):
                high, low = right[2 * i][:, cols], right[2 * i + 1][:, cols]
                rows = pl.ds(at, high.shape[0])
                at += high.shape[0]
                for term in (dot(lh[rows, :], high), dot(ll[rows, :], high), dot(lh[rows, :], low)):
                    total = term if total is None else total + term
            out[:, cols] = acc[:, cols] + total * scale

    else:
        ls, rs, held, sems = scratch
        depth = ls.shape[0] // 3
        for rows, value in pieces(slice(None)):
            high, low = split(value)
            for i, v in enumerate((high, low, high)):
                ls[pl.ds(i * depth + rows.start, 16), :] = v
        at = 0
        for i in range(len(parts)):
            size = right[2 * i].shape[0]
            for q, ref in enumerate((right[2 * i], right[2 * i], right[2 * i + 1])):
                rs[pl.ds(q * depth + at, size), :] = ref[...]
            at += size
        copies = []
        for j in range(n // TILE_N):
            cols = pl.ds(j * TILE_N, TILE_N)
            held[j] = acc[:, cols] + dot(ls[...], rs[:, cols]) * scale
            copies.append(pltpu.make_async_copy(held.at[j], out.at[:, cols], sems.at[j]))
            copies[-1].start()
        for copy in copies:
            copy.wait()


def add_product(acc, left, right, scale, place, last):
    m, n = acc.shape
    buffers, parts, rights = [], [], []
    for (half, group), classes in left.items():
        rights += right[half][2 * group : 2 * group + 2]
        for v in classes:
            if not any(v is u for u in buffers):
                buffers.append(v)
        parts.append((half, tuple(next(i for i, u in enumerate(buffers) if u is v) for v in classes)))
    total = sum(v.shape[0] for v in rights) // 2
    if last:
        tiles = n // TILE_N
        scratch = [pltpu.VMEM((3 * total, m), jnp.bfloat16), pltpu.VMEM((3 * total, n), jnp.bfloat16)]
        scratch += [pltpu.VMEM((tiles, m, TILE_N), jnp.float32), pltpu.SemaphoreType.DMA((tiles,))]
    else:
        scratch = [pltpu.VMEM((total, m), jnp.bfloat16)] * 2
    return pl.pallas_call(
        functools.partial(product_kernel, tuple(parts), len(buffers), scale, last),
        out_shape=jax.ShapeDtypeStruct(acc.shape, acc.dtype),
        in_specs=[pl.BlockSpec(memory_space=pltpu.SMEM)] + [INSIDE] * (1 + len(buffers) + len(rights)),
        out_specs=pl.BlockSpec(memory_space=pl.ANY) if last else INSIDE,
        scratch_shapes=scratch,
        cost_estimate=pl.CostEstimate(flops=6 * m * n * total, bytes_accessed=4 * total * (m + n) + 8 * m * n, transcendentals=0),
        compiler_params=pltpu.CompilerParams(vmem_limit_bytes=VMEM_BYTES),
    )(place, acc, *buffers, *rights)


def step(fisher, slab):
    scale = 1.0 / (slab.shape[0] * lax.axis_size("row") * lax.axis_size("col"))
    place = jnp.stack([lax.axis_index("row"), lax.axis_index("col")])

    s = exchange(slab, "row")
    d = exchange(slab, "col")
    zp, zm = send(s, dzh=1), send(s, dzh=-1)
    xp, xm = send(s, dx=1), send(s, dx=-1)
    x2 = relay(xp, xm, "dx")
    bpp, bmp = send(zp, dx=1), send(zp, dx=-1)
    bpm, bmm = send(zm, dx=1), send(zm, dx=-1)
    z2 = relay(zp, zm, "dzh")
    b2p, b2m = send(bpp, dx=1), send(bmm, dx=-1)
    cp, cm = send(z2, dx=1), send(z2, dx=-1)
    c2 = relay(cp, cm, "dx")

    dl = send(d, dzl=1)
    dp, dm = send(d, dy=1), send(d, dy=-1)
    lp, lm = send(dl, dy=1), send(dl, dy=-1)
    d2, l2 = relay(dp, dm, "dy"), relay(lp, lm, "dy")
    right = {}
    for half, own in enumerate([(d, dp, dm, d2), (dl, lp, lm, l2)]):
        pieces = []
        for value in own:
            pieces += [value, send(value, dk=1)]
        right[half] = prepare(pieces, place)

    first = [s, xp, xm, x2, zp, zm, bpp, bmp, bpm, bmm, z2]
    second = [b2p, b2m, cp, cm]
    third = [c2]
    calls = {
        "m1a": {(0, 0): first},
        "m1b": {(1, 0): first, (1, 1): second, (0, 1): second},
        "m2": {(0, 2): third, (1, 2): third},
    }
    acc = fisher
    for name, left in calls.items():
        acc = add_product(acc, left, right, scale, place, name == "m2")
    return acc


def solution(mesh):
    return jax.shard_map(
        step,
        mesh=mesh,
        in_specs=(P("row", "col"), P(("row", "col"), None)),
        out_specs=P("row", "col"),
        check_vma=False,
    )
```

```python
import functools

import jax
import jax.numpy as jnp
from jax import lax
from jax.experimental import pallas as pl
from jax.experimental.pallas import tpu as pltpu
from jax.sharding import PartitionSpec as P


AXES = ("row", "col")
TILE_N = 512
VMEM_BYTES = 14 << 20
INSIDE = pl.BlockSpec(memory_space=pltpu.VMEM)

SOURCES = (
    [(0, 0), (1, 0), (-1, 0), (2, 0), (0, 1), (0, -1), (1, 1), (-1, 1), (1, -1), (-1, -1), (0, 2)],
    [(2, 1), (2, -1), (1, 2), (-1, 2)],
    [(2, 2)],
)

STEPS = (0, 1, -1, 2)


def send(value, dy=0, dzl=0, dk=0, dx=0, dzh=0):
    def of(offset, k):
        return offset[k] if isinstance(offset, tuple) else offset

    pairs = []
    for y in range(4):
        for zl in range(2):
            for k in range(2):
                for x in range(4):
                    for zh in range(4):
                        here = (y * 4 + zl * 2 + k) * 16 + x * 4 + zh
                        there = (((y + of(dy, k)) % 4) * 4 + (zl ^ dzl) * 2 + (k ^ dk)) * 16
                        there += ((x + of(dx, k)) % 4) * 4 + (zh + of(dzh, k)) % 4
                        pairs.append((there, here))
    return lax.ppermute(value, AXES, pairs)


def relay(plus, minus, axis):
    value = jnp.where(lax.axis_index("row") & 1 == 0, plus, minus)
    return send(value, **{axis: (1, -1)})


def row_exchange(slab):
    rows, order = slab.shape
    n = lax.axis_size("row")
    got = lax.all_to_all(slab.reshape(rows, n, order // n), "row", split_axis=1, concat_axis=1, tiled=True)
    return got.transpose(1, 0, 2)


def col_exchange(slab):
    rows, order = slab.shape
    c = lax.axis_index("col")
    x, zh = c >> 2, c & 3
    tile = order // 16
    held = []
    for dx in STEPS:
        piece = lax.dynamic_slice_in_dim(slab, ((x - dx) & 3) * (4 * tile), 4 * tile, axis=1)
        piece = piece.reshape(rows, 4, tile).transpose(1, 0, 2)
        held.append(send(piece, dx=dx) if dx else piece)
    held = jnp.stack(held)
    got = []
    for dzh in STEPS:
        piece = lax.dynamic_slice_in_dim(held, (zh - dzh) & 3, 1, axis=1)[:, 0]
        got.append(send(piece, dzh=dzh) if dzh else piece)
    return jnp.concatenate(got, axis=0)


def split(value):
    high = value.astype(jnp.bfloat16)
    return high, (value - high.astype(jnp.float32)).astype(jnp.bfloat16)


def prepare_kernel(*refs):
    pieces, outs = refs[:8], refs[8:]
    width = 256

    @pl.loop(0, pieces[0].shape[2] // width)
    def _(j):
        cols = pl.ds(pl.multiple_of(j * width, width), width)
        for group, sources in enumerate(SOURCES):
            high, low = outs[2 * group : 2 * group + 2]
            for b, (dx, dzh) in enumerate(sources):
                at = STEPS.index(dzh) * 4 + STEPS.index(dx)
                for i in range(4):
                    rows = pl.ds(b * 64 + i * 16, 16)
                    both = jnp.concatenate([pieces[2 * i][at, :, cols], pieces[2 * i + 1][at, :, cols]], axis=0)
                    high[rows, cols], low[rows, cols] = split(both)


def prepare(pieces):
    m = pieces[0].shape[2]
    ks = [64 * len(sources) for sources in SOURCES for _ in range(2)]
    return pl.pallas_call(
        prepare_kernel,
        out_shape=[jax.ShapeDtypeStruct((k, m), jnp.bfloat16) for k in ks],
        in_specs=[INSIDE] * len(pieces),
        out_specs=[INSIDE] * len(ks),
        cost_estimate=pl.CostEstimate(flops=2 * sum(ks) * m, bytes_accessed=4 * sum(ks) * m, transcendentals=0),
        compiler_params=pltpu.CompilerParams(vmem_limit_bytes=VMEM_BYTES),
    )(*pieces)


def product_kernel(parts, n_left, scale, last, place, acc, *refs):
    left, right = refs[:n_left], refs[n_left : n_left + 2 * len(parts)]
    out, *scratch = refs[n_left + 2 * len(parts) :]
    m, n = acc.shape
    width = 256
    dims = (((0,), (0,)), ((), ()))
    dot = functools.partial(lax.dot_general, dimension_numbers=dims, preferred_element_type=jnp.float32)

    r = place[0]
    y, k = r >> 2, r & 1

    def pieces(cols):
        at = 0
        for half, classes in parts:
            zl = ((r >> 1) & 1) ^ half
            for which in classes:
                for dy in STEPS:
                    group = ((y + dy) & 3) * 4 + zl * 2
                    both = [left[which][group + (k ^ dk), :, cols] for dk in (0, 1)]
                    yield pl.ds(at, 16), jnp.concatenate(both, axis=0)
                    at += 16

    if not last:
        lh, ll = scratch

        @pl.loop(0, m // width)
        def _(j):
            cols = pl.ds(pl.multiple_of(j * width, width), width)
            for rows, value in pieces(cols):
                lh[rows, cols], ll[rows, cols] = split(value)

        @pl.loop(0, n // TILE_N)
        def _(j):
            cols = pl.ds(pl.multiple_of(j * TILE_N, TILE_N), TILE_N)
            at, total = 0, None
            for i in range(len(parts)):
                high, low = right[2 * i][:, cols], right[2 * i + 1][:, cols]
                rows = pl.ds(at, high.shape[0])
                at += high.shape[0]
                for term in (dot(lh[rows, :], high), dot(ll[rows, :], high), dot(lh[rows, :], low)):
                    total = term if total is None else total + term
            out[:, cols] = acc[:, cols] + total * scale

    else:
        ls, rs, held, sems = scratch
        depth = ls.shape[0] // 3
        for rows, value in pieces(slice(None)):
            high, low = split(value)
            for i, v in enumerate((high, low, high)):
                ls[pl.ds(i * depth + rows.start, 16), :] = v
        at = 0
        for i in range(len(parts)):
            size = right[2 * i].shape[0]
            for q, ref in enumerate((right[2 * i], right[2 * i], right[2 * i + 1])):
                rs[pl.ds(q * depth + at, size), :] = ref[...]
            at += size
        copies = []
        for j in range(n // TILE_N):
            cols = pl.ds(j * TILE_N, TILE_N)
            held[j] = acc[:, cols] + dot(ls[...], rs[:, cols]) * scale
            copies.append(pltpu.make_async_copy(held.at[j], out.at[:, cols], sems.at[j]))
            copies[-1].start()
        for copy in copies:
            copy.wait()


def add_product(acc, left, right, scale, place, last):
    m, n = acc.shape
    buffers, parts, rights = [], [], []
    for (half, group), classes in left.items():
        rights += right[half][2 * group : 2 * group + 2]
        for v in classes:
            if not any(v is u for u in buffers):
                buffers.append(v)
        parts.append((half, tuple(next(i for i, u in enumerate(buffers) if u is v) for v in classes)))
    total = sum(v.shape[0] for v in rights) // 2
    if last:
        tiles = n // TILE_N
        scratch = [pltpu.VMEM((3 * total, m), jnp.bfloat16), pltpu.VMEM((3 * total, n), jnp.bfloat16)]
        scratch += [pltpu.VMEM((tiles, m, TILE_N), jnp.float32), pltpu.SemaphoreType.DMA((tiles,))]
    else:
        scratch = [pltpu.VMEM((total, m), jnp.bfloat16)] * 2
    return pl.pallas_call(
        functools.partial(product_kernel, tuple(parts), len(buffers), scale, last),
        out_shape=jax.ShapeDtypeStruct(acc.shape, acc.dtype),
        in_specs=[pl.BlockSpec(memory_space=pltpu.SMEM)] + [INSIDE] * (1 + len(buffers) + len(rights)),
        out_specs=pl.BlockSpec(memory_space=pl.ANY) if last else INSIDE,
        scratch_shapes=scratch,
        cost_estimate=pl.CostEstimate(flops=6 * m * n * total, bytes_accessed=4 * total * (m + n) + 8 * m * n, transcendentals=0),
        compiler_params=pltpu.CompilerParams(vmem_limit_bytes=VMEM_BYTES),
    )(place, acc, *buffers, *rights)


def step(fisher, slab):
    scale = 1.0 / (slab.shape[0] * lax.axis_size("row") * lax.axis_size("col"))
    place = lax.axis_index("row")[None]

    s = row_exchange(slab)
    d = col_exchange(slab)
    zp, zm = send(s, dzh=1), send(s, dzh=-1)
    xp, xm = send(s, dx=1), send(s, dx=-1)
    x2 = relay(xp, xm, "dx")
    bpp, bmp = send(zp, dx=1), send(zp, dx=-1)
    bpm, bmm = send(zm, dx=1), send(zm, dx=-1)
    z2 = relay(zp, zm, "dzh")
    b2p, b2m = send(bpp, dx=1), send(bmm, dx=-1)
    cp, cm = send(z2, dx=1), send(z2, dx=-1)
    c2 = relay(cp, cm, "dx")

    dl = send(d, dzl=1)
    dp, dm = send(d, dy=1), send(d, dy=-1)
    lp, lm = send(dl, dy=1), send(dl, dy=-1)
    d2, l2 = relay(dp, dm, "dy"), relay(lp, lm, "dy")
    right = {}
    for half, own in enumerate([(d, dp, dm, d2), (dl, lp, lm, l2)]):
        pieces = []
        for value in own:
            pieces += [value, send(value, dk=1)]
        right[half] = prepare(pieces)

    first = [s, xp, xm, x2, zp, zm, bpp, bmp, bpm, bmm, z2]
    second = [b2p, b2m, cp, cm]
    third = [c2]
    calls = {
        "m1a": {(0, 0): first},
        "m1c": {(0, 1): second},
        "m1b": {(1, 0): first, (1, 1): second},
        "m2": {(0, 2): third, (1, 2): third},
    }
    acc = fisher
    for name, left in calls.items():
        acc = add_product(acc, left, right, scale, place, name == "m2")
    return acc


def solution(mesh):
    return jax.shard_map(
        step,
        mesh=mesh,
        in_specs=(P("row", "col"), P(("row", "col"), None)),
        out_specs=P("row", "col"),
        check_vma=False,
    )
```

```python
import functools

import jax
import jax.numpy as jnp
from jax import lax
from jax.experimental import pallas as pl
from jax.experimental.pallas import tpu as pltpu
from jax.sharding import PartitionSpec as P


AXES = ("row", "col")
TILE_N = 512
LAST_TILE_N = 256
VMEM_BYTES = 14 << 20
INSIDE = pl.BlockSpec(memory_space=pltpu.VMEM)

SOURCES = [(0, 0), (1, 0), (-1, 0), (2, 0), (0, 1), (0, -1), (1, 1), (-1, 1), (1, -1), (-1, -1), (0, 2)]
SOURCES += [(2, 1), (2, -1), (1, 2), (-1, 2), (2, 2)]
PARTS = ((0, (0, 1, -1, 2), (11, 4, 1)), (1, (0, 1, -1), (10, 5, 1)), (1, (2,), (15, 1)))
PRODUCTS = {"m1a": [(0, 0)], "m1b": [(1, 0)], "m1c": [(0, 1)], "m1d": [(1, 1), (2, 0)], "m2": [(0, 2), (1, 2), (2, 1)]}

STEPS = (0, 1, -1, 2)


def send(value, dy=0, dzl=0, dk=0, dx=0, dzh=0):
    def of(offset, k):
        return offset[k] if isinstance(offset, tuple) else offset

    pairs = []
    for y in range(4):
        for zl in range(2):
            for k in range(2):
                for x in range(4):
                    for zh in range(4):
                        here = (y * 4 + zl * 2 + k) * 16 + x * 4 + zh
                        there = (((y + of(dy, k)) % 4) * 4 + (zl ^ dzl) * 2 + (k ^ dk)) * 16
                        there += ((x + of(dx, k)) % 4) * 4 + (zh + of(dzh, k)) % 4
                        pairs.append((there, here))
    return lax.ppermute(value, AXES, pairs)


def relay(plus, minus, axis):
    value = jnp.where(lax.axis_index("row") & 1 == 0, plus, minus)
    return send(value, **{axis: (1, -1)})


def row_exchange(slab):
    rows, order = slab.shape
    n = lax.axis_size("row")
    got = lax.all_to_all(slab.reshape(rows, n, order // n), "row", split_axis=1, concat_axis=1, tiled=True)
    return got.transpose(1, 0, 2)


def col_exchange(slab):
    rows, order = slab.shape
    c = lax.axis_index("col")
    x, zh = c >> 2, c & 3
    tile = order // 16
    held = []
    for dx in STEPS:
        piece = lax.dynamic_slice_in_dim(slab, ((x - dx) & 3) * (4 * tile), 4 * tile, axis=1)
        piece = piece.reshape(rows, 4, tile).transpose(1, 0, 2)
        held.append(send(piece, dx=dx) if dx else piece)
    held = jnp.stack(held)
    got = []
    for dzh in STEPS:
        piece = lax.dynamic_slice_in_dim(held, (zh - dzh) & 3, 1, axis=1)[:, 0]
        got.append(send(piece, dzh=dzh) if dzh else piece)
    return jnp.concatenate(got, axis=0)


def split(value):
    high = value.astype(jnp.bfloat16)
    return high, (value - high.astype(jnp.float32)).astype(jnp.bfloat16)


def prepare_kernel(part, *refs):
    _, dys, counts = PARTS[part]
    pieces, outs = refs[: 2 * len(dys)], refs[2 * len(dys) :]
    width = 256

    @pl.loop(0, pieces[0].shape[2] // width)
    def _(j):
        cols = pl.ds(pl.multiple_of(j * width, width), width)
        first = 0
        for group, count in enumerate(counts):
            high, low = outs[2 * group : 2 * group + 2]
            for b, (dx, dzh) in enumerate(SOURCES[first : first + count]):
                at = STEPS.index(dzh) * 4 + STEPS.index(dx)
                for i in range(len(dys)):
                    rows = pl.ds((b * len(dys) + i) * 16, 16)
                    both = jnp.concatenate([pieces[2 * i][at, :, cols], pieces[2 * i + 1][at, :, cols]], axis=0)
                    high[rows, cols], low[rows, cols] = split(both)
            first += count


def prepare(pieces, part):
    m = pieces[0].shape[2]
    _, dys, counts = PARTS[part]
    ks = [16 * len(dys) * count for count in counts for _ in range(2)]
    return pl.pallas_call(
        functools.partial(prepare_kernel, part),
        out_shape=[jax.ShapeDtypeStruct((k, m), jnp.bfloat16) for k in ks],
        in_specs=[INSIDE] * len(pieces),
        out_specs=[INSIDE] * len(ks),
        cost_estimate=pl.CostEstimate(flops=2 * sum(ks) * m, bytes_accessed=4 * sum(ks) * m, transcendentals=0),
        compiler_params=pltpu.CompilerParams(vmem_limit_bytes=VMEM_BYTES),
    )(*pieces)


def product_kernel(parts, n_left, scale, last, place, acc, *refs):
    left, right = refs[:n_left], refs[n_left : n_left + 2 * len(parts)]
    out, *scratch = refs[n_left + 2 * len(parts) :]
    m, n = acc.shape
    width = 256
    dims = (((0,), (0,)), ((), ()))
    dot = functools.partial(lax.dot_general, dimension_numbers=dims, preferred_element_type=jnp.float32)

    r = place[0]
    y, k = r >> 2, r & 1

    def pieces(cols):
        at = 0
        for part, classes in parts:
            half, dys, _ = PARTS[part]
            zl = ((r >> 1) & 1) ^ half
            for which in classes:
                for dy in dys:
                    group = ((y + dy) & 3) * 4 + zl * 2
                    both = [left[which][group + (k ^ dk), :, cols] for dk in (0, 1)]
                    yield pl.ds(at, 16), jnp.concatenate(both, axis=0)
                    at += 16

    if not last:
        lh, ll = scratch

        @pl.loop(0, m // width)
        def _(j):
            cols = pl.ds(pl.multiple_of(j * width, width), width)
            for rows, value in pieces(cols):
                lh[rows, cols], ll[rows, cols] = split(value)

        @pl.loop(0, n // TILE_N)
        def _(j):
            cols = pl.ds(pl.multiple_of(j * TILE_N, TILE_N), TILE_N)
            at, total = 0, None
            for i in range(len(parts)):
                high, low = right[2 * i][:, cols], right[2 * i + 1][:, cols]
                rows = pl.ds(at, high.shape[0])
                at += high.shape[0]
                for term in (dot(lh[rows, :], high), dot(ll[rows, :], high), dot(lh[rows, :], low)):
                    total = term if total is None else total + term
            out[:, cols] = acc[:, cols] + total * scale

    else:
        ls, rs, held, sems = scratch
        depth = ls.shape[0] // 3
        for rows, value in pieces(slice(None)):
            high, low = split(value)
            for i, v in enumerate((high, low, high)):
                ls[pl.ds(i * depth + rows.start, 16), :] = v
        at = 0
        for i in range(len(parts)):
            size = right[2 * i].shape[0]
            for q, ref in enumerate((right[2 * i], right[2 * i], right[2 * i + 1])):
                rs[pl.ds(q * depth + at, size), :] = ref[...]
            at += size
        copies = []
        for j in range(n // LAST_TILE_N):
            cols = pl.ds(j * LAST_TILE_N, LAST_TILE_N)
            held[j] = acc[:, cols] + dot(ls[...], rs[:, cols]) * scale
            copies.append(pltpu.make_async_copy(held.at[j], out.at[:, cols], sems.at[j]))
            copies[-1].start()
        for copy in copies:
            copy.wait()


def add_product(acc, left, right, scale, place, last):
    m, n = acc.shape
    buffers, parts, rights = [], [], []
    for (part, group), classes in left.items():
        rights += right[part][2 * group : 2 * group + 2]
        for v in classes:
            if not any(v is u for u in buffers):
                buffers.append(v)
        parts.append((part, tuple(next(i for i, u in enumerate(buffers) if u is v) for v in classes)))
    total = sum(v.shape[0] for v in rights) // 2
    if last:
        tiles = n // LAST_TILE_N
        scratch = [pltpu.VMEM((3 * total, m), jnp.bfloat16), pltpu.VMEM((3 * total, n), jnp.bfloat16)]
        scratch += [pltpu.VMEM((tiles, m, LAST_TILE_N), jnp.float32), pltpu.SemaphoreType.DMA((tiles,))]
    else:
        scratch = [pltpu.VMEM((total, m), jnp.bfloat16)] * 2
    return pl.pallas_call(
        functools.partial(product_kernel, tuple(parts), len(buffers), scale, last),
        out_shape=jax.ShapeDtypeStruct(acc.shape, acc.dtype),
        in_specs=[pl.BlockSpec(memory_space=pltpu.SMEM)] + [INSIDE] * (1 + len(buffers) + len(rights)),
        out_specs=pl.BlockSpec(memory_space=pl.ANY) if last else INSIDE,
        scratch_shapes=scratch,
        cost_estimate=pl.CostEstimate(flops=6 * m * n * total, bytes_accessed=4 * total * (m + n) + 8 * m * n, transcendentals=0),
        compiler_params=pltpu.CompilerParams(vmem_limit_bytes=VMEM_BYTES),
    )(place, acc, *buffers, *rights)


def step(fisher, slab):
    scale = 1.0 / (slab.shape[0] * lax.axis_size("row") * lax.axis_size("col"))
    place = lax.axis_index("row")[None]

    s = row_exchange(slab)
    d = col_exchange(slab)
    zp, zm = send(s, dzh=1), send(s, dzh=-1)
    xp, xm = send(s, dx=1), send(s, dx=-1)
    x2 = relay(xp, xm, "dx")
    bpp, bmp = send(zp, dx=1), send(zp, dx=-1)
    bpm, bmm = send(zm, dx=1), send(zm, dx=-1)
    z2 = relay(zp, zm, "dzh")
    b2p, b2m = send(bpp, dx=1), send(bmm, dx=-1)
    cp, cm = send(z2, dx=1), send(z2, dx=-1)
    c2 = relay(cp, cm, "dx")

    dl = send(d, dzl=1)
    dp, dm = send(d, dy=1), send(d, dy=-1)
    lp, lm = send(dl, dy=1), send(dl, dy=-1)
    d2, l2 = relay(dp, dm, "dy"), relay(lp, lm, "dy")
    right = []
    swaps = {}
    for half, own in enumerate([(d, dp, dm, d2), (dl, lp, lm, l2)]):
        for i, value in enumerate(own):
            swaps[half, STEPS[i]] = [value, send(value, dk=1)]
    for part, (half, dys, _) in enumerate(PARTS):
        right.append(prepare([v for dy in dys for v in swaps[half, dy]], part))

    sources = [s, xp, xm, x2, zp, zm, bpp, bmp, bpm, bmm, z2, b2p, b2m, cp, cm, c2]
    acc = fisher
    for name, wanted in PRODUCTS.items():
        left = {}
        for part, group in wanted:
            counts = PARTS[part][2]
            first = sum(counts[:group])
            left[part, group] = sources[first : first + counts[group]]
        acc = add_product(acc, left, right, scale, place, name == "m2")
    return acc


def solution(mesh):
    return jax.shard_map(
        step,
        mesh=mesh,
        in_specs=(P("row", "col"), P(("row", "col"), None)),
        out_specs=P("row", "col"),
        check_vma=False,
    )
```
